256 devices in a mesh: gx: 8 (over z), gy: 16 (over y, x), gz: 2 (over core).
Axes of the slice: x: 4, y: 4, z: 8, core: 2. Of those that a mesh axis runs over, the one named last changes fastest.
Arguments:
- bin_mass: float32 [8, 16, 12, 8, 8, 8, 128], P('gx', 'gy', 'gz'), may hold values from 0.1 to 1
- wind_field: float32 [8, 16, 12, 2, 8, 64], P('gx', 'gy', 'gz'), may hold values from -0.3 to 0.3
- fall_speed: float32 [128], replicated, may hold values from 0.02 to 0.4
- gain_a: float32 [128, 128], replicated, may hold values from -0.5 to 0.5
- gain_b: float32 [128, 128], replicated, may hold values from -0.5 to 0.5
- gain_c: float32 [128, 128], replicated, may hold values from -0.5 to 0.5
- loss_k: float32 [128, 128], replicated, may hold values from -0.5 to 0.5
- old_occupied: int32 [8, 16, 6], P('gx', 'gy'), may hold values from 0 to 1, as said below
- old_neighbours: int32 [8, 16, 6, 4], P('gx', 'gy'), may hold values from -1 to 8, as said below
- old_sends: int32 [8, 16, 4, 3], P('gx', 'gy'), may hold values from -1 to 5, as said below
- old_substeps: int32 [1, 8, 16, 12], P(None, 'gx', 'gy', 'gz'), may hold values from 1 to 4
- move_lists: int32 [8, 16, 3, 2], P('gx', 'gy'), may hold values from -1 to 5, as said below
- new_sources: int32 [8, 16, 6], P('gx', 'gy'), may hold values from -1 to 11, as said below
- new_neighbours: int32 [8, 16, 6, 4], P('gx', 'gy'), may hold values from -1 to 8, as said below
- new_sends: int32 [8, 16, 4, 3], P('gx', 'gy'), may hold values from -1 to 5, as said below
- new_substeps: int32 [1, 8, 16, 12], P(None, 'gx', 'gy', 'gz'), may hold values from 1 to 4
Outputs:
- final_mass: float32 [8, 16, 12, 8, 8, 8, 128], P('gx', 'gy', 'gz')
The draws below stay inside these ranges and needn't reach their ends.
Inputs may be any that keep to these rules, and one draw needn't show every extreme that they name: `old_occupied`: slots marked 1 hold blocks before the move; some position has all 6 marked. `old_neighbours`: -1 marks the domain's edge or an empty slot; a value under 6 is a slot of the same device; a value 6 + k is entry k of the list that the device next on that side keeps for the opposite side. Lists before and after the move are consistent with each other and with the send lists. `old_sends`: entries are occupied slots of the device, -1 pads; some list holds 3 entries. `move_lists`: entries are occupied old slots, each block sent at most once, -1 pads; routes 0 and 1 each hold 2 entries on some device. `new_sources`: -1 marks an empty slot; a value under 6 is an own old slot that stays; 6 + r * 2 + k is entry k of route r of the sending device; every block has exactly one new slot. `new_neighbours`: as old_neighbours, for the layout after the move. `new_sends`: as old_sends, for the layout after the move.
All inputs are finite; a program needn't handle non-finite values.
Results may differ from the reference program's by a relative error of at most 0.0003.
Values sent between devices are 32-bit elements; how exact they have to be, the bound alone decides.
No kernel may reach another device: no remote copies, remote signals or barrier semaphores. Data moves between devices by JAX's collectives and lax.ppermute only.
A program may use at most 64 MiB of HBM per device.

```python
import math
import jax
import jax.numpy as jnp
from jax import lax

BINS = 128
BX = 8
BY = 8
BZ = 8
TX = 2
TY = 2
SMAX = 4
HALF_STEPS = 1
SLOTS = 6
FCAP = 3
MCAP = 2
N_GX = 8
N_GY = 16
N_GZ = 2


def relabel_codes(codes, rank):
    flat = codes.reshape(N_GX, N_GY, -1)
    mapped = jnp.take_along_axis(rank, jnp.clip(flat, 0, SLOTS - 1), axis=2)
    return jnp.where((flat >= 0) & (flat < SLOTS), mapped, flat).reshape(codes.shape).astype(jnp.int32)


def layout_lists(key):
    key_x, key_y, key_p, key_q = jax.random.split(jax.random.fold_in(key, 7), 4)
    col_index = jnp.arange(N_GX, dtype=jnp.int32)
    row_index = jnp.arange(N_GY, dtype=jnp.int32)
    mid_x = N_GX // 2
    mid_y = N_GY // 2
    force_x = (col_index == 0) | (col_index == mid_x) | (col_index == N_GX - 2) | (col_index == mid_x - 1) & (N_GX > 4)
    force_y = (row_index == 0) | (row_index == mid_y - 1) | (row_index == mid_y) | (row_index == N_GY - 2) | (row_index == mid_y - 2) & (N_GY > 4)
    move_x = jax.random.randint(key_x, (N_GX,), 0, 2).astype(jnp.int32)
    move_x = jnp.where(col_index == N_GX - 1, 0, jnp.where(force_x, 1, move_x))
    move_y = jax.random.randint(key_y, (N_GY,), 0, 2).astype(jnp.int32)
    move_y = jnp.where(row_index == N_GY - 1, 0, jnp.where(force_y, 1, move_y))
    prev_x = jnp.concatenate([jnp.zeros((1,), jnp.int32), move_x[:-1]])
    prev_y = jnp.concatenate([jnp.zeros((1,), jnp.int32), move_y[:-1]])
    width_cols = TX + prev_x - move_x
    height = TY + prev_y - move_y
    full_shape = (N_GX, N_GY, SLOTS)
    dev_i = jnp.broadcast_to(col_index[:, None, None], full_shape)
    dev_j = jnp.broadcast_to(row_index[None, :, None], full_shape)
    slot_index = jnp.broadcast_to(jnp.arange(SLOTS, dtype=jnp.int32)[None, None, :], full_shape)
    width_dev = width_cols[dev_i]
    height_dev = height[dev_j]
    col_a = slot_index // TY
    row_r = slot_index % TY
    old_live = slot_index < width_dev * TY
    west_code = jnp.where(col_a > 0, slot_index - TY, jnp.where(dev_i == 0, -1, SLOTS + row_r))
    east_code = jnp.where(col_a < width_dev - 1, slot_index + TY, jnp.where(dev_i == N_GX - 1, -1, SLOTS + row_r))
    south_code = jnp.where(row_r > 0, slot_index - 1, jnp.where(dev_j == 0, -1, SLOTS + col_a))
    north_code = jnp.where(row_r < TY - 1, slot_index + 1, jnp.where(dev_j == N_GY - 1, -1, SLOTS + col_a))
    old_neighbours = jnp.where(old_live[..., None], jnp.stack([west_code, east_code, south_code, north_code], axis=-1), -1).astype(jnp.int32)
    send_shape = (N_GX, N_GY, FCAP)
    entry_index = jnp.broadcast_to(jnp.arange(FCAP, dtype=jnp.int32)[None, None, :], send_shape)
    at_i = jnp.broadcast_to(col_index[:, None, None], send_shape)
    at_j = jnp.broadcast_to(row_index[None, :, None], send_shape)
    wide_cols = width_cols[at_i]
    tall_rows = height[at_j]
    send_west = jnp.where((entry_index < TY) & (at_i > 0), entry_index, -1)
    send_east = jnp.where((entry_index < TY) & (at_i < N_GX - 1), (wide_cols - 1) * TY + entry_index, -1)
    send_south = jnp.where((entry_index < wide_cols) & (at_j > 0), entry_index * TY, -1)
    send_north = jnp.where((entry_index < wide_cols) & (at_j < N_GY - 1), entry_index * TY + TY - 1, -1)
    old_sends = jnp.stack([send_west, send_east, send_south, send_north], axis=2).astype(jnp.int32)
    row_b = slot_index // TX
    col_c = slot_index % TX
    new_live = slot_index < height_dev * TX
    west_code = jnp.where(col_c > 0, slot_index - 1, jnp.where(dev_i == 0, -1, SLOTS + row_b))
    east_code = jnp.where(col_c < TX - 1, slot_index + 1, jnp.where(dev_i == N_GX - 1, -1, SLOTS + row_b))
    south_code = jnp.where(row_b > 0, slot_index - TX, jnp.where(dev_j == 0, -1, SLOTS + col_c))
    north_code = jnp.where(row_b < height_dev - 1, slot_index + TX, jnp.where(dev_j == N_GY - 1, -1, SLOTS + col_c))
    new_neighbours = jnp.where(new_live[..., None], jnp.stack([west_code, east_code, south_code, north_code], axis=-1), -1).astype(jnp.int32)
    send_west = jnp.where((entry_index < tall_rows) & (at_i > 0), entry_index * TX, -1)
    send_east = jnp.where((entry_index < tall_rows) & (at_i < N_GX - 1), entry_index * TX + TX - 1, -1)
    send_south = jnp.where((entry_index < TX) & (at_j > 0), entry_index, -1)
    send_north = jnp.where((entry_index < TX) & (at_j < N_GY - 1), (tall_rows - 1) * TX + entry_index, -1)
    new_sends = jnp.stack([send_west, send_east, send_south, send_north], axis=2).astype(jnp.int32)
    block_x = dev_i * TX - prev_x[dev_i] + col_a
    block_y = dev_j * TY + row_r
    tile_x = jnp.clip(block_x // TX, 0, N_GX - 1)
    move_bx = (move_x[tile_x] == 1) & (block_x % TX == TX - 1)
    move_by = (move_y[dev_j] == 1) & (row_r == TY - 1)
    route_dir = jnp.where(move_bx & move_by, 2, jnp.where(move_bx, 0, jnp.where(move_by, 1, 3)))
    route_dir = jnp.where(old_live, route_dir, 3).astype(jnp.int32)
    route_hot = (route_dir[..., None] == jnp.arange(4, dtype=jnp.int32)[None, None, None, :]).astype(jnp.int32)
    route_rank = jnp.sum((jnp.cumsum(route_hot, axis=2) - route_hot) * route_hot, axis=-1).astype(jnp.int32)
    full_lists = jnp.full((N_GX, N_GY, 4, SLOTS), -1, jnp.int32).at[dev_i, dev_j, route_dir, route_rank].set(slot_index)
    move_lists = full_lists[:, :, :3, :MCAP]
    dest_j = jnp.clip(dev_j + move_by.astype(jnp.int32), 0, N_GY - 1)
    low_y = dest_j * TY - prev_y[dest_j]
    dest_slot = jnp.where(old_live, (block_y - low_y) * TX + (block_x - tile_x * TX), SLOTS).astype(jnp.int32)
    source_code = jnp.where(route_dir == 3, slot_index, SLOTS + route_dir * MCAP + route_rank).astype(jnp.int32)
    sources = jnp.full((N_GX, N_GY, SLOTS + 1), -1, jnp.int32).at[tile_x, dest_j, dest_slot].set(source_code)
    new_sources = sources[:, :, :SLOTS]
    scores = jax.random.randint(key_p, full_shape, 0, 4096).astype(jnp.int32) * SLOTS + slot_index
    order = jnp.argsort(scores, axis=2).astype(jnp.int32)
    rank = jnp.argsort(order, axis=2).astype(jnp.int32)
    old_neighbours = relabel_codes(old_neighbours, rank)
    old_neighbours = jnp.take_along_axis(old_neighbours, jnp.broadcast_to(order[..., None], old_neighbours.shape), axis=2).astype(jnp.int32)
    old_sends = relabel_codes(old_sends, rank)
    move_lists = relabel_codes(move_lists, rank)
    new_sources = relabel_codes(new_sources, rank)
    old_occupied = jnp.take_along_axis(old_live.astype(jnp.int32), order, axis=2).astype(jnp.int32)
    new_scores = jax.random.randint(key_q, full_shape, 0, 4096).astype(jnp.int32) * SLOTS + slot_index
    new_order = jnp.argsort(new_scores, axis=2).astype(jnp.int32)
    new_rank = jnp.argsort(new_order, axis=2).astype(jnp.int32)
    new_neighbours = relabel_codes(new_neighbours, new_rank)
    new_neighbours = jnp.take_along_axis(new_neighbours, jnp.broadcast_to(new_order[..., None], new_neighbours.shape), axis=2).astype(jnp.int32)
    new_sends = relabel_codes(new_sends, new_rank)
    new_sources = jnp.take_along_axis(new_sources, new_order, axis=2).astype(jnp.int32)
    return (old_occupied, old_neighbours, old_sends, move_lists, new_sources, new_neighbours, new_sends)


def draw_old_occupied(key, part):
    return layout_lists(key)[0]


def draw_old_neighbours(key, part):
    return layout_lists(key)[1]


def draw_old_sends(key, part):
    return layout_lists(key)[2]


def draw_move_lists(key, part):
    return layout_lists(key)[3]


def draw_new_sources(key, part):
    return layout_lists(key)[4]


def draw_new_neighbours(key, part):
    return layout_lists(key)[5]


def draw_new_sends(key, part):
    return layout_lists(key)[6]


def touch_ends(entries, own_key, smallest, top_value):
    place = [jax.random.randint(jax.random.fold_in(own_key, axis), (), 0, length) for axis, length in enumerate(entries.shape)]
    main_axis = entries.shape.index(max(entries.shape))
    beside = place[:main_axis] + [(place[main_axis] + 1) % entries.shape[main_axis]] + place[main_axis + 1:]
    return entries.at[tuple(place)].set(smallest).at[tuple(beside)].set(top_value)


def steps_of(own_key, extent, shards, least, high):
    factor_of, own = 1.0, jax.random.fold_in(own_key, 6)
    for dim, shards_of in shards:
        steps = jnp.exp(jax.random.uniform(jax.random.fold_in(own, dim), (shards_of,), jnp.float32, least / len(shards), high / len(shards)))
        factor_of = factor_of * jnp.repeat(steps, extent[dim] // shards_of).reshape([-1 if axis == dim else 1 for axis in range(len(extent))])
    return factor_of


def scatter_about(key, shape, width, bound, held_as=jnp.bfloat16):
    return jnp.clip(width * jax.random.normal(key, shape, jnp.float32), -bound, bound).astype(held_as)


def setup_inputs(seed: int = 0) -> dict:
    keys = jax.random.split(jax.random.key(seed), 17)
    bin_mass = jnp.clip(0.1 + 0.9 * jax.random.uniform(keys[0], (N_GX, N_GY, N_GZ * SLOTS, BX, BY, BZ, BINS), jnp.float32) ** steps_of(keys[0], (N_GX, N_GY, N_GZ * SLOTS, BX, BY, BZ, BINS), ((0, 8), (1, 16), (2, 2)), -0.2, 0.2), 0.1, 1.0)
    wind_field = jnp.clip(jax.random.uniform(keys[1], (N_GX, N_GY, N_GZ * SLOTS, 2, BX, BY * BZ), jnp.float32, -0.3, 0.3) * steps_of(keys[1], (N_GX, N_GY, N_GZ * SLOTS, 2, BX, BY * BZ), ((0, 8), (1, 16), (2, 2)), -0.4, 0.0), -0.3, 0.3)
    fall_speed = jnp.clip(jnp.exp(jax.random.uniform(keys[2], (BINS,), jnp.float32, math.log(0.02), math.log(0.4))), 0.02, 0.4)
    gain_a = scatter_about(keys[3], (BINS, BINS), BINS ** -0.5, 0.5, jnp.float32)
    gain_b = scatter_about(keys[4], (BINS, BINS), BINS ** -0.5, 0.5, jnp.float32)
    gain_c = scatter_about(keys[5], (BINS, BINS), BINS ** -0.5, 0.5, jnp.float32)
    loss_k = scatter_about(keys[6], (BINS, BINS), BINS ** -0.5, 0.5, jnp.float32)
    old_occupied = draw_old_occupied(jax.random.fold_in(keys[16], 71), 0)
    old_neighbours = draw_old_neighbours(jax.random.fold_in(keys[16], 71), 0)
    old_sends = draw_old_sends(jax.random.fold_in(keys[16], 71), 0)
    old_substeps = touch_ends(jax.random.randint(keys[10], (HALF_STEPS, N_GX, N_GY, N_GZ * SLOTS), 1, SMAX + 1), jax.random.fold_in(keys[10], 1), 1, SMAX).astype(jnp.int32)
    move_lists = draw_move_lists(jax.random.fold_in(keys[16], 71), 0)
    new_sources = draw_new_sources(jax.random.fold_in(keys[16], 71), 0)
    new_neighbours = draw_new_neighbours(jax.random.fold_in(keys[16], 71), 0)
    new_sends = draw_new_sends(jax.random.fold_in(keys[16], 71), 0)
    new_substeps = touch_ends(jax.random.randint(keys[15], (HALF_STEPS, N_GX, N_GY, N_GZ * SLOTS), 1, SMAX + 1), jax.random.fold_in(keys[15], 1), 1, SMAX).astype(jnp.int32)
    return dict(bin_mass=bin_mass, wind_field=wind_field, fall_speed=fall_speed, gain_a=gain_a, gain_b=gain_b, gain_c=gain_c, loss_k=loss_k, old_occupied=old_occupied, old_neighbours=old_neighbours, old_sends=old_sends, old_substeps=old_substeps, move_lists=move_lists, new_sources=new_sources, new_neighbours=new_neighbours, new_sends=new_sends, new_substeps=new_substeps)


step_time = 0.25


def coag_tendency(mass_field, gain_a, gain_b, gain_c, loss_k):
    exact_mode = lax.Precision.HIGHEST
    first_map = jnp.matmul(mass_field, gain_a, precision=exact_mode, preferred_element_type=jnp.float32)
    second_map = jnp.matmul(mass_field, gain_b, precision=exact_mode, preferred_element_type=jnp.float32)
    gained = jnp.matmul(first_map * second_map, gain_c, precision=exact_mode, preferred_element_type=jnp.float32)
    lost_mass = mass_field * jnp.matmul(mass_field, loss_k, precision=exact_mode, preferred_element_type=jnp.float32)
    return gained - lost_mass


def advect(mass_field, speed_x, speed_y, west_mass, west_speed, east_mass, east_speed, south_mass, south_speed, north_mass, north_speed, from_above, fall_speed):
    padded_x = jnp.concatenate([west_mass[..., None, :, :, :], mass_field, east_mass[..., None, :, :, :]], axis=-4)
    wind_x = jnp.concatenate([west_speed[..., None, :, :], speed_x, east_speed[..., None, :, :]], axis=-3)[..., None]
    flux_x = jnp.maximum(wind_x[..., :-1, :, :, :], 0.0) * padded_x[..., :-1, :, :, :] + jnp.minimum(wind_x[..., 1:, :, :, :], 0.0) * padded_x[..., 1:, :, :, :]
    padded_y = jnp.concatenate([south_mass[..., :, None, :, :], mass_field, north_mass[..., :, None, :, :]], axis=-3)
    wind_y = jnp.concatenate([south_speed[..., :, None, :], speed_y, north_speed[..., :, None, :]], axis=-2)[..., None]
    flux_y = jnp.maximum(wind_y[..., :, :-1, :, :], 0.0) * padded_y[..., :, :-1, :, :] + jnp.minimum(wind_y[..., :, 1:, :, :], 0.0) * padded_y[..., :, 1:, :, :]
    upper_mass = jnp.concatenate([mass_field[..., :, :, 1:, :], from_above[..., :, :, None, :]], axis=-2)
    return mass_field - (flux_x[..., 1:, :, :, :] - flux_x[..., :-1, :, :, :]) - (flux_y[..., :, 1:, :, :] - flux_y[..., :, :-1, :, :]) - fall_speed * (mass_field - upper_mass)


def face_sources(neighbours, sends, face_side):
    shift_i = (-1, 1, 0, 0)[face_side]
    shift_j = (0, 0, -1, 1)[face_side]
    opposite = (1, 0, 3, 2)[face_side]
    entry_code = neighbours[:, :, :, face_side]
    rows_i = jnp.arange(N_GX, dtype=jnp.int32)[:, None, None]
    rows_j = jnp.arange(N_GY, dtype=jnp.int32)[None, :, None]
    near_i = jnp.clip(rows_i + shift_i, 0, N_GX - 1)
    near_j = jnp.clip(rows_j + shift_j, 0, N_GY - 1)
    entry_index = jnp.clip(entry_code - SLOTS, 0, FCAP - 1)
    remote = sends[near_i, near_j, opposite, entry_index]
    is_local = entry_code < SLOTS
    source_i = jnp.where(is_local, rows_i, near_i)
    source_j = jnp.where(is_local, rows_j, near_j)
    source_s = jnp.clip(jnp.where(is_local, entry_code, remote), 0, SLOTS - 1)
    valid = (entry_code >= 0) & (is_local | (remote >= 0))
    return source_i, source_j, source_s, valid


def update_blocks(items, fall_speed, weights):
    mass_field, speed_x, speed_y = items[0], items[1], items[2]
    face_data = items[3:11]
    from_above, counts = items[11], items[12]
    advected = advect(mass_field, speed_x, speed_y, face_data[0], face_data[1], face_data[2], face_data[3], face_data[4], face_data[5], face_data[6], face_data[7], from_above, fall_speed)
    step_size = step_time / jnp.maximum(counts, 1).astype(jnp.float32)
    step_scale = step_size[..., None, None, None, None]
    for turn_index in range(SMAX):
        active = (turn_index < counts)[..., None, None, None, None]
        advected = jnp.where(active, advected + step_scale * coag_tendency(advected, weights[0], weights[1], weights[2], weights[3]), advected)
    return advected


def advance(mass_grid, wind_grid, neighbours, sends, counts, fall_speed, weights):
    speed_x = wind_grid[:, :, :, :, 0]
    speed_y = wind_grid[:, :, :, :, 1]
    layers = ((mass_grid[:, :, :, :, -1], speed_x[:, :, :, :, -1]), (mass_grid[:, :, :, :, 0], speed_x[:, :, :, :, 0]),
              (mass_grid[:, :, :, :, :, -1], speed_y[:, :, :, :, :, -1]), (mass_grid[:, :, :, :, :, 0], speed_y[:, :, :, :, :, 0]))
    levels = jnp.arange(N_GZ, dtype=jnp.int32)[None, None, :, None]
    face_data = []
    for face_side in range(4):
        source_i, source_j, source_s, valid = face_sources(neighbours, sends, face_side)
        picker = (source_i[:, :, None, :], source_j[:, :, None, :], levels, source_s[:, :, None, :])
        kept_mask = valid[:, :, None, :]
        layer_mass, layer_speed = layers[face_side]
        face_data.append(jnp.where(kept_mask[..., None, None, None], layer_mass[picker], 0.0))
        face_data.append(jnp.where(kept_mask[..., None, None], layer_speed[picker], 0.0))
    from_above = jnp.concatenate([mass_grid[:, :, 1:, :, :, :, 0], jnp.zeros_like(mass_grid[:, :, :1, :, :, :, 0])], axis=2)

    def per_column(items):
        return update_blocks(items, fall_speed, weights)

    return lax.map(per_column, (mass_grid, speed_x, speed_y) + tuple(face_data) + (from_above, counts))


def migrate(mass_grid, wind_grid, new_sources, move_lists):
    rows_i = jnp.arange(N_GX, dtype=jnp.int32)[:, None, None]
    rows_j = jnp.arange(N_GY, dtype=jnp.int32)[None, :, None]
    is_local = new_sources < SLOTS
    offset = jnp.clip(new_sources - SLOTS, 0, 3 * MCAP - 1)
    route_dir = offset // MCAP
    entry_index = offset % MCAP
    near_i = jnp.clip(rows_i + jnp.where(route_dir == 1, 0, 1), 0, N_GX - 1)
    near_j = jnp.clip(rows_j + jnp.where(route_dir == 0, 0, -1), 0, N_GY - 1)
    remote = move_lists[near_i, near_j, route_dir, entry_index]
    source_i = jnp.where(is_local, rows_i, near_i)
    source_j = jnp.where(is_local, rows_j, near_j)
    source_s = jnp.clip(jnp.where(is_local, new_sources, remote), 0, SLOTS - 1)
    levels = jnp.arange(N_GZ, dtype=jnp.int32)[None, None, :, None]
    picker = (source_i[:, :, None, :], source_j[:, :, None, :], levels, source_s[:, :, None, :])
    kept_mask = (new_sources >= 0)[:, :, None, :]
    moved_mass = jnp.where(kept_mask[..., None, None, None, None], mass_grid[picker], 0.0)
    moved_wind = jnp.where(kept_mask[..., None, None, None, None], wind_grid[picker], 0.0)
    return moved_mass, moved_wind


def reference(bin_mass, wind_field, fall_speed, gain_a, gain_b, gain_c, loss_k, old_occupied, old_neighbours, old_sends, old_substeps, move_lists, new_sources, new_neighbours, new_sends, new_substeps):
    weights = (gain_a, gain_b, gain_c, loss_k)
    mass_grid = bin_mass.reshape(N_GX, N_GY, N_GZ, SLOTS, BX, BY, BZ, BINS)
    wind_grid = wind_field.reshape(N_GX, N_GY, N_GZ, SLOTS, 2, BX, BY, BZ)
    occupied = (old_occupied > 0)[:, :, None, :]
    mass_grid = jnp.where(occupied[..., None, None, None, None], mass_grid, 0.0)
    before = old_substeps.reshape(HALF_STEPS, N_GX, N_GY, N_GZ, SLOTS)
    after = new_substeps.reshape(HALF_STEPS, N_GX, N_GY, N_GZ, SLOTS)
    for step_index in range(HALF_STEPS):
        mass_grid = advance(mass_grid, wind_grid, old_neighbours, old_sends, before[step_index], fall_speed, weights)
    mass_grid, wind_grid = migrate(mass_grid, wind_grid, new_sources, move_lists)
    for step_index in range(HALF_STEPS):
        mass_grid = advance(mass_grid, wind_grid, new_neighbours, new_sends, after[step_index], fall_speed, weights)
    return mass_grid.reshape(N_GX, N_GY, N_GZ * SLOTS, BX, BY, BZ, BINS)
```

```python
import jax
import jax.numpy as jnp
from jax import lax
from jax.experimental import pallas as pl
from jax.experimental.pallas import tpu as pltpu
from jax.sharding import PartitionSpec as P

f32 = jnp.float32
bf16 = jnp.bfloat16
SLOTS, BINS, CELLS, FACE = 6, 128, 512, 64
FCAP, MCAP = 3, 2
MOVED_ROWS = CELLS + 16 + 8
VMEM = pl.BlockSpec(memory_space=pltpu.VMEM)
SMEM = pl.BlockSpec(memory_space=pltpu.SMEM)


def shape_of(*dims, dtype=f32):
    return jax.ShapeDtypeStruct(dims, dtype)


def call(body, outs, operands, scratch=(), flops=0, aliases=None, limit=24 << 20):
    scalar_count = sum(1 for _, kind in operands if kind == "s")
    bytes_moved = sum(4 * a.size for a, _ in operands) + sum(4 * o.size for o in outs)
    return pl.pallas_call(
        body,
        out_shape=list(outs),
        in_specs=[SMEM if kind == "s" else VMEM for _, kind in operands],
        out_specs=[VMEM] * len(outs),
        scratch_shapes=list(scratch),
        input_output_aliases=aliases or {},
        compiler_params=pltpu.CompilerParams(vmem_limit_bytes=limit),
        cost_estimate=pl.CostEstimate(
            flops=flops, bytes_accessed=bytes_moved, transcendentals=0
        ),
    )(*[a for a, _ in operands])


def turned(wind_ref, wt_ref, tmp_ref):
    for slot in range(SLOTS):
        tmp_ref[:, 0:64] = wind_ref[slot]
        wt_ref[slot] = jnp.transpose(tmp_ref[...])[0:64, :]


def lanes(column, rows):
    return jnp.broadcast_to(column, (rows, BINS))


def west_face(mass_ref, wt_ref, slot):
    return jnp.minimum(lanes(wt_ref[slot, :, 0:1], 64), 0.0) * mass_ref[slot, 0:64, :]


def east_face(mass_ref, wt_ref, slot):
    return jnp.maximum(lanes(wt_ref[slot, :, 7:8], 64), 0.0) * mass_ref[slot, 448:512, :]


def south_face(mass_ref, wt_ref, slot):
    return [
        jnp.minimum(lanes(wt_ref[slot, 0:8, 8 + x : 9 + x], 8), 0.0)
        * mass_ref[slot, x * 64 : x * 64 + 8, :]
        for x in range(8)
    ]


def north_face(mass_ref, wt_ref, slot):
    return [
        jnp.maximum(lanes(wt_ref[slot, 56:64, 8 + x : 9 + x], 8), 0.0)
        * mass_ref[slot, x * 64 + 56 : x * 64 + 64, :]
        for x in range(8)
    ]


def pack_faces(sends_ref, mass_ref, wt_ref, to_w, to_e, to_s, to_n):
    def entry(k, carry):
        for side, out in enumerate((to_w, to_e, to_s, to_n)):
            code = sends_ref[0, 0, side, k]
            slot = jnp.maximum(code, 0)
            keep = code >= 0
            if side == 0:
                out[k] = jnp.where(keep, west_face(mass_ref, wt_ref, slot), 0.0)
            elif side == 1:
                out[k] = jnp.where(keep, east_face(mass_ref, wt_ref, slot), 0.0)
            else:
                tiles = (south_face if side == 2 else north_face)(mass_ref, wt_ref, slot)
                for x in range(8):
                    out[k, x * 8 : x * 8 + 8, :] = jnp.where(keep, tiles[x], 0.0)
        return carry

    lax.fori_loop(0, FCAP, entry, 0)


def first_pack(occ, sends, mass, wind, to_w, to_e, to_s, to_n, down, wt, tmp):
    tmp[...] = jnp.zeros_like(tmp)
    turned(wind, wt, tmp)
    pack_faces(sends, mass, wt, to_w, to_e, to_s, to_n)
    for slot in range(SLOTS):
        bottom = mass[slot, pl.ds(0, FACE, stride=8), :]
        down[slot] = jnp.where(occ[0, 0, slot] > 0, bottom, 0.0)


def fill_candidates(mass, wt, live, received, cand):
    for side in range(4):
        cand[side, SLOTS + FCAP] = jnp.zeros((FACE, BINS), f32)
        cand[side, SLOTS : SLOTS + FCAP] = received[side][...]

    def local(slot, carry):
        keep = live(slot)
        cand[0, slot] = jnp.where(keep, east_face(mass, wt, slot), 0.0)
        cand[1, slot] = jnp.where(keep, west_face(mass, wt, slot), 0.0)
        north = north_face(mass, wt, slot)
        south = south_face(mass, wt, slot)
        for x in range(8):
            cand[2, slot, x * 8 : x * 8 + 8, :] = jnp.where(keep, north[x], 0.0)
            cand[3, slot, x * 8 : x * 8 + 8, :] = jnp.where(keep, south[x], 0.0)
        return carry

    lax.fori_loop(0, SLOTS, local, 0)


def advect_slot(mass, wt, above, fall, neighbours, cand, slot, out):
    codes = [neighbours[0, 0, slot, side] for side in range(4)]
    picks = [jnp.where(code < 0, SLOTS + FCAP, code) for code in codes]
    fall_row = lanes(fall[...], 64) if fall.shape[0] == 64 else jnp.broadcast_to(fall[...], (64, BINS))
    top = lax.broadcasted_iota(jnp.int32, (64, BINS), 0) % 8 == 7
    upwind_before = cand[0, picks[0]]
    held = None
    for x in range(8):
        here = mass[slot, x * 64 : x * 64 + 64, :]
        u = lanes(wt[slot, :, x : x + 1], 64)
        v = lanes(wt[slot, :, 8 + x : 9 + x], 64)
        plus_x = jnp.maximum(u, 0.0) * here
        if x < 7:
            after = jnp.minimum(lanes(wt[slot, :, x + 1 : x + 2], 64), 0.0) * mass[
                slot, x * 64 + 64 : x * 64 + 128, :
            ]
        else:
            after = cand[1, picks[1]]
        minus_x = held if held is not None else jnp.minimum(u, 0.0) * here
        plus_y = jnp.maximum(v, 0.0) * here
        minus_y = jnp.minimum(v, 0.0) * here
        south = cand[2, picks[2], x * 8 : x * 8 + 8, :]
        north = cand[3, picks[3], x * 8 : x * 8 + 8, :]
        plus_before = jnp.concatenate([south, plus_y[0:56]], axis=0)
        minus_after = jnp.concatenate([minus_y[8:64], north], axis=0)
        lid = above[slot, x * 8 : x * 8 + 8, :]
        lid = jnp.broadcast_to(lid[:, None, :], (8, 8, BINS)).reshape(64, BINS)
        upper = jnp.where(top, lid, pltpu.roll(here, 63, 0))
        out[slot, x * 64 : x * 64 + 64, :] = (
            here
            - ((plus_x + after) - (upwind_before + minus_x))
            - ((plus_y + minus_after) - (plus_before + minus_y))
            - fall_row * (here - upper)
        )
        upwind_before = plus_x
        held = after


def first_advect(
    occ, neighbours, counts, move, mass, wind, wt, fall, rw, re, rs, rn, above,
    ga, gb, gc, lk,
    out, go_w, go_n, go_c, w1, w2, w3, w4, cand,
):
    fill_candidates(mass, wt, lambda slot: occ[0, 0, slot] > 0, (rw, re, rs, rn), cand)

    def one(slot, carry):
        @pl.when(occ[0, 0, slot] > 0)
        def _():
            advect_slot(mass, wt, above, fall, neighbours, cand, slot, out)

        return carry

    lax.fori_loop(0, SLOTS, one, 0)
    for route, target in enumerate((go_w, go_n, go_c)):
        for k in range(MCAP):
            code = move[0, 0, route, k]

            @pl.when(code >= 0)
            def _():
                target[k, 0:CELLS, :] = out[code]
                target[k, CELLS : CELLS + 16, 0:64] = wind[code]
                target[k, CELLS + 16 : CELLS + 24, :] = jnp.full(
                    (8, BINS), counts[0, 0, 0, code].astype(f32)
                )

    split_weights(ga, gb, gc, lk, w1, w2, w3, w4)


def halves(x):
    high = x.astype(bf16)
    return high, (x - high.astype(f32)).astype(bf16)


def split_weights(ga, gb, gc, lk, w1, w2, w3, w4):
    ah, al = halves(ga[...])
    bh, bl = halves(gb[...])
    ch, cl = halves(gc[...])
    kh, kl = halves(lk[...])
    nothing = jnp.zeros_like(al)
    for row in (0, 128):
        w1[row : row + 128, 0:128] = ah
        w1[row : row + 128, 128:256] = bh
        w2[row : row + 128, 0:128] = kh
        w2[row : row + 128, 128:256] = al if row == 0 else nothing
        w4[row : row + 128, 0:128] = ch
        w4[row : row + 128, 128:256] = cl if row == 0 else nothing
    w3[:, 0:128] = bl
    w3[:, 128:256] = kl


def coagulate(state, slot, turns, w1, w2, w3, w4):
    step = jnp.where(
        turns <= 1, 0.25, jnp.where(turns == 2, 0.125, jnp.where(turns == 3, 0.25 / 3, 0.0625))
    ).astype(f32)

    def turn(_, carry):
        x = state[slot]
        xh, xl = halves(x)
        both = jnp.concatenate([xh, xl], axis=1)
        o1 = jnp.dot(both, w1[...], preferred_element_type=f32)
        o2 = jnp.dot(both, w2[...], preferred_element_type=f32)
        o3 = jnp.dot(xh, w3[...], preferred_element_type=f32)
        first = o1[:, 0:128] + o2[:, 128:256]
        second = o1[:, 128:256] + o3[:, 0:128]
        lost = o2[:, 0:128] + o3[:, 128:256]
        ph, plo = halves(first * second)
        o4 = jnp.dot(jnp.concatenate([ph, plo], axis=1), w4[...], preferred_element_type=f32)
        state[slot] = x + step * ((o4[:, 0:128] + o4[:, 128:256]) - x * lost)
        return carry

    lax.fori_loop(0, turns, turn, 0)


def stay_coag(sources, counts, moved, w1, w2, w3, w4, out):
    def one(slot, carry):
        code = sources[0, 0, slot]

        @pl.when(jnp.logical_and(code >= 0, code < SLOTS))
        def _():
            out[slot] = moved[code]
            coagulate(out, slot, counts[0, 0, 0, code], w1, w2, w3, w4)

        return carry

    lax.fori_loop(0, SLOTS, one, 0)


def arrive_coag(
    sources, sends, held, old_wind, from_w, from_n, from_c, w1, w2, w3, w4,
    out, to_w, to_e, to_s, to_n, down, wt, wind, tmp,
):
    tmp[...] = jnp.zeros_like(tmp)

    def one(slot, carry):
        code = sources[0, 0, slot]

        @pl.when(code < 0)
        def _():
            out[slot] = jnp.zeros((CELLS, BINS), f32)
            wind[slot] = jnp.zeros((16, 64), f32)

        @pl.when(jnp.logical_and(code >= 0, code < SLOTS))
        def _():
            wind[slot] = old_wind[code]

        for route, source in enumerate((from_w, from_n, from_c)):
            k = code - SLOTS - route * MCAP

            @pl.when(jnp.logical_and(k >= 0, k < MCAP))
            def _():
                out[slot] = source[k, 0:CELLS, :]
                wind[slot] = source[k, CELLS : CELLS + 16, 0:64]
                turns = jnp.max(source[k, CELLS + 16 : CELLS + 24, :]).astype(jnp.int32)
                coagulate(out, slot, turns, w1, w2, w3, w4)

        return carry

    lax.fori_loop(0, SLOTS, one, 0)
    turned(wind, wt, tmp)
    pack_faces(sends, out, wt, to_w, to_e, to_s, to_n)
    for slot in range(SLOTS):
        down[slot] = out[slot, pl.ds(0, FACE, stride=8), :]


def second_step(
    sources, neighbours, counts, mass, wt, fall, rw, re, rs, rn, above, w1, w2, w3, w4, out, cand
):
    fill_candidates(mass, wt, lambda slot: sources[0, 0, slot] >= 0, (rw, re, rs, rn), cand)

    def one(slot, carry):
        live = sources[0, 0, slot] >= 0

        @pl.when(live)
        def _():
            advect_slot(mass, wt, above, fall, neighbours, cand, slot, out)
            coagulate(out, slot, counts[0, 0, 0, slot], w1, w2, w3, w4)

        @pl.when(jnp.logical_not(live))
        def _():
            out[slot] = jnp.zeros((CELLS, BINS), f32)

        return carry

    lax.fori_loop(0, SLOTS, one, 0)


def sent(block, axis, distance):
    size = lax.axis_size(axis)
    return lax.ppermute(
        block, axis, [(i, i + distance) for i in range(size) if 0 <= i + distance < size]
    )


def sent_corner(block):
    nx, ny = lax.axis_size("gx"), lax.axis_size("gy")
    pairs = [
        (i * ny + j, (i - 1) * ny + j + 1) for i in range(1, nx) for j in range(ny - 1)
    ]
    return lax.ppermute(block, ("gx", "gy"), pairs)


def exchange(to_w, to_e, to_s, to_n, down):
    from_e = sent(to_w, "gx", -1)
    from_w = sent(to_e, "gx", 1)
    from_n = sent(to_s, "gy", -1)
    from_s = sent(to_n, "gy", 1)
    above = sent(down, "gz", -1)
    return from_w, from_e, from_s, from_n, above


def on_device(
    bin_mass, wind_field, fall_speed, gain_a, gain_b, gain_c, loss_k,
    old_occupied, old_neighbours, old_sends, old_substeps, move_lists, new_sources,
    new_neighbours, new_sends, new_substeps,
):
    mass = bin_mass.reshape(SLOTS, CELLS, BINS)
    wind = wind_field.reshape(SLOTS, 16, 64)
    fall = fall_speed.reshape(1, BINS)
    face = shape_of(FCAP, FACE, BINS)
    lid = shape_of(SLOTS, FACE, BINS)
    blocks = shape_of(SLOTS, CELLS, BINS)
    turned_wind = shape_of(SLOTS, 64, 16)
    moved = shape_of(MCAP, MOVED_ROWS, BINS)
    wide = [shape_of(256, 256, dtype=bf16)] * 2 + [
        shape_of(128, 256, dtype=bf16), shape_of(256, 256, dtype=bf16)
    ]
    tmp = pltpu.VMEM((16, 128), f32)
    cand = pltpu.VMEM((4, SLOTS + FCAP + 1, FACE, BINS), f32)
    unit = 2 * CELLS * 256 * 256 * 4

    *packed, wt = call(
        first_pack,
        [face] * 4 + [lid, turned_wind],
        [(old_occupied, "s"), (old_sends, "s"), (mass, "v"), (wind, "v")],
        scratch=[tmp],
    )
    got = exchange(*packed)
    vectors = [mass, wind, wt, fall, *got, gain_a, gain_b, gain_c, loss_k]
    advected, go_w, go_n, go_c, *weights = call(
        first_advect,
        [blocks, moved, moved, moved] + wide,
        [(old_occupied, "s"), (old_neighbours, "s"), (old_substeps, "s"), (move_lists, "s")]
        + [(a, "v") for a in vectors],
        scratch=[cand],
    )
    from_w = sent(go_w, "gx", -1)
    from_n = sent(go_n, "gy", 1)
    from_c = sent_corner(go_c)
    (stayed,) = call(
        stay_coag,
        [blocks],
        [(new_sources, "s"), (old_substeps, "s")] + [(a, "v") for a in [advected, *weights]],
        flops=unit * 10,
    )
    state, *packed, wt = call(
        arrive_coag,
        [blocks] + [face] * 4 + [lid, turned_wind],
        [(new_sources, "s"), (new_sends, "s")]
        + [(a, "v") for a in [stayed, wind, from_w, from_n, from_c, *weights]],
        scratch=[pltpu.VMEM((SLOTS, 16, 64), f32), tmp],
        flops=unit * 5,
        aliases={2: 0},
    )
    got = exchange(*packed)
    (final,) = call(
        second_step,
        [blocks],
        [(new_sources, "s"), (new_neighbours, "s"), (new_substeps, "s")]
        + [(a, "v") for a in [state, wt, fall, *got, *weights]],
        scratch=[cand],
        flops=unit * 10,
    )
    return final.reshape(bin_mass.shape)


def solution(mesh):
    placed = (
        P("gx", "gy", "gz", None, None, None, None),
        P("gx", "gy", "gz", None, None, None),
        P(),
        P(),
        P(),
        P(),
        P(),
        P("gx", "gy", None),
        P("gx", "gy", None, None),
        P("gx", "gy", None, None),
        P(None, "gx", "gy", "gz"),
        P("gx", "gy", None, None),
        P("gx", "gy", None),
        P("gx", "gy", None, None),
        P("gx", "gy", None, None),
        P(None, "gx", "gy", "gz"),
    )
    return jax.shard_map(
        on_device,
        mesh=mesh,
        in_specs=placed,
        out_specs=P("gx", "gy", "gz", None, None, None, None),
        check_vma=False,
    )
```
